32 devices in a mesh: wide: 4 (over x, core), narrow: 8 (over z, y).
Axes of the slice: x: 2, y: 2, z: 4, core: 2. Of those that a mesh axis runs over, the one named last changes fastest.
Arguments:
- photo_embeds: bfloat16 [8192, 1152], P(('wide', 'narrow')), may hold values from -2.5 to 2.5
- caption_vectors: bfloat16 [8192, 1152], P(('wide', 'narrow')), may hold values from -2.5 to 2.5
- positive_match_index: int32 [8192], P(('wide', 'narrow')), may hold values from 0 to 1023
- trained_logscale_param: float32 [1], replicated, may hold values from 2 to 8
- offset_bias_array: float32 [1], replicated, may hold values from -4 to -1
Outputs:
- grad_images: float32 [8192, 1152], P(('wide', 'narrow'))
- grad_texts: float32 [8192, 1152], P(('wide', 'narrow'))
The draws below stay inside these ranges and needn't reach their ends.
Inputs may be any that keep to these rules, and one draw needn't show every extreme that they name: `positive_match_index`: labels of an image name one of the 1024 texts that its block meets, s * 256 + j for column j of the block met at step s.
All inputs are finite; a program needn't handle non-finite values.
Results may differ from the reference program's by a relative error of at most 0.0022.
Values may be sent and summed in bfloat16 or wider, within the bound.
A program may use at most 64 MiB of HBM per device.

```python
import math
import jax
import jax.numpy as jnp

D = 1152
B = 256
STEPS = 4
PAIRS = 8192


def set_ends(drawn, own_key, smallest, top_value):
    longest = drawn.shape.index(max(drawn.shape))
    spots = []
    for shift in (0, 1):
        where = [jax.random.randint(jax.random.fold_in(own_key, axis), (), 0, length) for axis, length in enumerate(drawn.shape)]
        where[longest] = (where[longest] + shift) % drawn.shape[longest]
        spots.append(tuple(where))
    return drawn.at[spots[0]].set(smallest).at[spots[1]].set(top_value)


def steps_of(rng, dims, split, least, top_value):
    gain, own = 1.0, jax.random.fold_in(rng, 6)
    for axis_at, blocks in split:
        heights = jnp.exp(jax.random.uniform(jax.random.fold_in(own, axis_at), (blocks,), jnp.float32, least / len(split), top_value / len(split)))
        gain = gain * jnp.repeat(heights, dims[axis_at] // blocks).reshape([-1 if axis == axis_at else 1 for axis in range(len(dims))])
    return gain


def bell_draw(own_key, shape, width, bound, split=(), held_as=jnp.bfloat16):
    values = jax.random.normal(own_key, shape, jnp.float32) * width
    if len(split) > 0:
        values = steps_of(own_key, shape, split, -0.22, 0.18) * values
    return jnp.clip(values, min=-bound, max=bound).astype(held_as)


def setup_inputs(seed: int = 0) -> dict:
    key_list = jax.random.split(jax.random.key(seed), 6)
    return {
        "photo_embeds": bell_draw(key_list[0], (PAIRS, D), 0.17, 2.5, ((0, 32),)),
        "caption_vectors": bell_draw(key_list[1], (PAIRS, D), 0.17, 2.5, ((0, 32),)),
        "positive_match_index": set_ends(jax.random.randint(key_list[2], (PAIRS,), 0, STEPS * B), jax.random.fold_in(key_list[2], 1), 0, (STEPS * B) - 1).astype(jnp.int32),
        "trained_logscale_param": jnp.clip(jnp.exp(jax.random.uniform(key_list[3], (1,), jnp.float32, math.log(2.0), math.log(8.0))), 2.0, 8.0),
        "offset_bias_array": jnp.clip(jax.random.uniform(key_list[4], (1,), jnp.float32, -4.0, -1.0), -4.0, -1.0),
    }


def reference(photo_embeds, caption_vectors, positive_match_index, trained_logscale_param, offset_bias_array):
    count = photo_embeds.shape[0] // B
    photo_groups = photo_embeds.reshape(count, B, D).astype(jnp.float32)
    text_blocks = caption_vectors.reshape(count, B, D).astype(jnp.float32)
    label_block_stack = positive_match_index.reshape(count, B)
    exp_sharpening_coefficient = trained_logscale_param[0]
    derivative_photo_embeds = jnp.zeros((count, B, D), jnp.float32)
    grad_txt = jnp.zeros((count, B, D), jnp.float32)
    matched_entries = jnp.arange(B, dtype=jnp.int32)
    for step in range(STEPS):
        encountered = jnp.roll(text_blocks, step, axis=0)
        pairwise_score = exp_sharpening_coefficient * jnp.einsum("ufg,ucg->ufc", photo_groups, encountered) + offset_bias_array[0]
        target_sign_matrix = label_block_stack[:, :, None] == (matched_entries + step * B)[None, None, :]
        sign = jnp.where(target_sign_matrix, 1.0, -1.0).astype(jnp.float32)
        derivative_weighting = (-sign * jax.nn.sigmoid(-sign * pairwise_score)).astype(jnp.bfloat16).astype(jnp.float32)
        derivative_photo_embeds = derivative_photo_embeds + exp_sharpening_coefficient * jnp.einsum("alu,auo->alo", derivative_weighting, encountered)
        incomplete_sentence_derivative = exp_sharpening_coefficient * jnp.einsum("gep,geo->gpo", derivative_weighting, photo_groups)
        grad_txt = grad_txt + jnp.roll(incomplete_sentence_derivative, -step, axis=0)
    return derivative_photo_embeds.reshape(count * B, D), grad_txt.reshape(count * B, D)
```

```python
import functools

import jax
import jax.numpy as jnp
from jax import lax
from jax.experimental import pallas as pl
from jax.experimental.pallas import tpu as pltpu
from jax.sharding import PartitionSpec as P

STEPS = 4
CHUNKS = 4
AHEAD = 2
LAG_Z = 3
LAG_Y = 0
PIECES = 2
MESH = pl.DeviceIdType.MESH


def slope_tile(left, right, labels, text_axis, first, scale, shift):
    score = scale * lax.dot_general(
        left, right, (((1,), (1,)), ((), ())), preferred_element_type=jnp.float32
    ) + shift
    match = labels == lax.broadcasted_iota(jnp.int32, score.shape, text_axis) + first
    half = jax.nn.sigmoid(jnp.where(match, -score, score))
    return jnp.where(match, -half, half).astype(jnp.bfloat16)


def kernel(
    wide,
    narrow,
    scale_ref,
    shift_ref,
    label_hbm,
    image_hbm,
    text_hbm,
    grad_image_ref,
    grad_text_ref,
    image_ref,
    text_ref,
    texts,
    images,
    labels,
    label_column,
    label_ref,
    loaded,
    text_arrival,
    image_arrival,
    label_arrival,
    departure,
    label_departure,
):
    devices = wide * narrow
    me = lax.axis_index("wide") * narrow + lax.axis_index("narrow")
    odd = lax.rem(me, 2)
    rows = image_ref.shape[0]
    part = rows // CHUNKS

    def place(by):
        at = lax.rem(me + by + devices, devices)
        return (lax.div(at, narrow), lax.rem(at, narrow))

    barrier = pltpu.get_barrier_semaphore()
    near = [by for s in range(1, STEPS) for by in (s, -s)]
    for by in near:
        pl.semaphore_signal(barrier, inc=1, device_id=place(by), device_id_type=MESH)
    loads = [
        pltpu.make_async_copy(src, dst, loaded.at[at])
        for at, (src, dst) in enumerate(
            (
                (image_hbm, image_ref),
                (text_hbm, text_ref),
                (label_hbm, label_ref),
            )
        )
    ]
    for load in loads:
        load.start()
    for load in loads:
        load.wait()
    pl.semaphore_wait(barrier, len(near))

    def label_copy(s):
        return pltpu.make_async_remote_copy(
            src_ref=label_ref,
            dst_ref=labels.at[s - 1],
            send_sem=label_departure.at[s - 1],
            recv_sem=label_arrival.at[s - 1],
            device_id=place(-s),
            device_id_type=MESH,
        )

    def routes(own_major, major, major_arrival, own_minor, minor, minor_arrival, d):
        def send(lane, src, dst, arrival, slot, by):
            def chunk(c):
                span = pl.ds(c * part, part)
                return pltpu.make_async_remote_copy(
                    src_ref=src.at[span],
                    dst_ref=dst.at[slot].at[span],
                    send_sem=departure.at[lane, c],
                    recv_sem=arrival.at[slot, c],
                    device_id=place(by),
                    device_id_type=MESH,
                )

            return chunk

        return (
            send(0, own_minor, minor, minor_arrival, 1, -2 * d),
            send(1, own_major, major, major_arrival, 1, 2 * d),
            send(2, own_major, major, major_arrival, 0, d),
            send(3, minor.at[1], minor, minor_arrival, 0, d),
            send(4, major.at[1], major, major_arrival, 2, d),
            send(5, major.at[0], major, major_arrival, 2, 2 * d),
        )

    text_side = (text_ref, texts, text_arrival)
    image_side = (image_ref, images, image_arrival)

    def both(body):
        @pl.when(odd == 0)
        def _():
            body(routes(*text_side, *image_side, 1), text_side, image_side)

        @pl.when(odd == 1)
        def _():
            body(routes(*image_side, *text_side, -1), image_side, text_side)

    def landed(side, slot, c):
        _, buffer, arrival = side
        here = buffer.at[slot].at[pl.ds(c * part, part)]
        pltpu.make_async_copy(here, here, arrival.at[slot, c]).wait()

    def begin(lanes, major, minor):
        for c in range(CHUNKS):
            lanes[0](c).start()
            lanes[1](c).start()
            if c < AHEAD:
                lanes[2](c).start()

    both(begin)
    for s in range(1, STEPS):
        label_copy(s).start()

    scale, shift = scale_ref[0], shift_ref[0]
    label_column[...] = jnp.broadcast_to(label_ref[...], (rows, rows)).T

    def image_share(s, at=0, size=rows):
        span = pl.ds(at, size)
        block = text_ref[span] if s == 0 else texts[s - 1, span]
        slope = slope_tile(
            image_ref[...], block, label_column[:, :size], 1, s * rows + at, scale, shift
        )
        return scale * jnp.dot(slope, block, preferred_element_type=jnp.float32)

    def text_share(s, at=0, size=rows):
        span = pl.ds(at, size)
        block = image_ref[span] if s == 0 else images[s - 1, span]
        own = label_ref[:, span] if s == 0 else labels[s - 1, :, span]
        slope = slope_tile(text_ref[...], block, own, 0, s * rows, scale, shift)
        return scale * jnp.dot(slope, block, preferred_element_type=jnp.float32)

    def relay(start, stop):
        def body(lanes, major, minor):
            for t in range(start, stop):
                if t < CHUNKS:
                    landed(minor, 1, t)
                    lanes[3](t).start()
                    if t + AHEAD < CHUNKS:
                        lanes[2](t + AHEAD).start()
                if 0 <= t - LAG_Z < CHUNKS:
                    landed(major, 0, t - LAG_Z)
                    lanes[5](t - LAG_Z).start()
                if 0 <= t - LAG_Y < CHUNKS:
                    landed(major, 1, t - LAG_Y)
                    lanes[4](t - LAG_Y).start()

        return body

    def add_text(s):
        grad_text_ref[...] += text_share(s)

    def add_image(s):
        grad_image_ref[...] += image_share(s)

    end = CHUNKS + max(LAG_Z, LAG_Y)
    both(relay(0, 2))
    grad_image_ref[...] = image_share(0)
    both(relay(2, 4))
    grad_text_ref[...] = text_share(0)
    both(relay(4, 5))
    for s in range(1, STEPS):
        label_copy(s).wait_recv()
    add_image(2)
    both(relay(5, 6))
    add_text(2)
    both(relay(6, end))

    def rest(lanes, major, minor):
        for c in range(CHUNKS):
            landed(minor, 0, c)

    both(rest)
    add_image(1)
    add_text(1)

    def last(lanes, major, minor):
        for c in range(CHUNKS):
            landed(minor, 2, c)
        (add_text if major is text_side else add_image)(STEPS - 1)
        for c in range(CHUNKS):
            landed(major, 2, c)

    both(last)

    def finish(lanes, major, minor):
        for lane in lanes:
            for c in range(CHUNKS):
                lane(c).wait_send()

    both(finish)
    for s in range(1, STEPS):
        label_copy(s).wait_send()


def tail_kernel(
    narrow,
    scale_ref,
    shift_ref,
    grad_image_ref,
    grad_text_ref,
    image_ref,
    text_ref,
    texts,
    images,
    labels,
    label_column,
    image_out,
    text_out,
    stage,
    stored,
):
    odd = lax.rem(lax.axis_index("wide") * narrow + lax.axis_index("narrow"), 2)
    scale, shift = scale_ref[0], shift_ref[0]
    rows = image_ref.shape[0]
    size, s = rows // PIECES, STEPS - 1

    def close(done, done_out, part_ref, out, own_ref, block_ref, slope_of):
        stores = [pltpu.make_async_copy(done, done_out, stored.at[PIECES])]
        stores[0].start()
        block = block_ref[s - 1]
        for piece in range(PIECES):
            span = pl.ds(piece * size, size)
            slope = slope_of(own_ref[span], block, piece * size, span)
            stage[span] = part_ref[span] + scale * jnp.dot(
                slope, block, preferred_element_type=jnp.float32
            )
            store = pltpu.make_async_copy(stage.at[span], out.at[span], stored.at[piece])
            store.start()
            stores.append(store)
        for store in stores:
            store.wait()

    @pl.when(odd == 0)
    def _():
        def slope_of(own, block, at, span):
            return slope_tile(own, block, label_column[span], 1, s * rows, scale, shift)

        close(grad_text_ref, text_out, grad_image_ref, image_out, image_ref, texts, slope_of)

    @pl.when(odd == 1)
    def _():
        def slope_of(own, block, at, span):
            return slope_tile(own, block, labels[s - 1], 0, s * rows + at, scale, shift)

        close(grad_image_ref, image_out, grad_text_ref, text_out, text_ref, images, slope_of)


def on_device(wide, narrow, photo, caption, match_index, logscale, offset):
    rows, width = photo.shape
    here = pl.BlockSpec(memory_space=pltpu.HBM)
    smem = pl.BlockSpec(memory_space=pltpu.SMEM)
    vmem = pl.BlockSpec(memory_space=pltpu.VMEM)
    operands = [
        pltpu.with_memory_space_constraint(array, pltpu.HBM)
        for array in (match_index.reshape(1, rows), photo, caption)
    ]
    held = (
        pltpu.VMEM((rows, width), jnp.float32),
        pltpu.VMEM((rows, width), jnp.float32),
        pltpu.VMEM((rows, width), jnp.bfloat16),
        pltpu.VMEM((rows, width), jnp.bfloat16),
        pltpu.VMEM((STEPS - 1, rows, width), jnp.bfloat16),
        pltpu.VMEM((STEPS - 1, rows, width), jnp.bfloat16),
        pltpu.VMEM((STEPS - 1, 1, rows), jnp.int32),
        pltpu.VMEM((rows, rows), jnp.int32),
    )
    tiles = 4 * STEPS * rows * rows * width
    results = pl.pallas_call(
        functools.partial(kernel, wide, narrow),
        out_shape=held,
        in_specs=[smem] * 2 + [here] * 3,
        out_specs=(vmem,) * len(held),
        scratch_shapes=[
            pltpu.VMEM((1, rows), jnp.int32),
            pltpu.SemaphoreType.DMA((3,)),
            pltpu.SemaphoreType.DMA((STEPS - 1, CHUNKS)),
            pltpu.SemaphoreType.DMA((STEPS - 1, CHUNKS)),
            pltpu.SemaphoreType.DMA((STEPS - 1,)),
            pltpu.SemaphoreType.DMA((6, CHUNKS)),
            pltpu.SemaphoreType.DMA((STEPS - 1,)),
        ],
        compiler_params=pltpu.CompilerParams(
            collective_id=0, has_side_effects=True, vmem_limit_bytes=32 * 1024 * 1024
        ),
        cost_estimate=pl.CostEstimate(
            flops=2 * tiles, bytes_accessed=6 * rows * width * 2, transcendentals=0
        ),
        name="sigmoid_ring",
    )(logscale, offset, *operands)
    out = jax.ShapeDtypeStruct((rows, width), jnp.float32)
    return pl.pallas_call(
        functools.partial(tail_kernel, narrow),
        out_shape=(out, out),
        in_specs=[smem] * 2 + [vmem] * len(held),
        out_specs=(here, here),
        scratch_shapes=[
            pltpu.VMEM((rows, width), jnp.float32),
            pltpu.SemaphoreType.DMA((PIECES + 1,)),
        ],
        compiler_params=pltpu.CompilerParams(vmem_limit_bytes=16 * 1024 * 1024),
        name="sigmoid_tail",
    )(logscale, offset, *results)


def solution(mesh):
    pairs = ("wide", "narrow")
    return jax.shard_map(
        functools.partial(on_device, mesh.shape["wide"], mesh.shape["narrow"]),
        mesh=mesh,
        in_specs=(P(pairs, None), P(pairs, None), P(pairs), P(), P()),
        out_specs=(P(pairs, None), P(pairs, None)),
        check_vma=False,
    )
```

```python
import functools

import jax
import jax.numpy as jnp
from jax import lax
from jax.experimental import pallas as pl
from jax.experimental.pallas import tpu as pltpu
from jax.sharding import PartitionSpec as P

STEPS = 4
CHUNKS = 4
AHEAD = 2
PIECES = 1
HEAD = 0
MESH = pl.DeviceIdType.MESH


def slope_tile(left, right, labels, text_axis, first, scale, shift):
    score = scale * lax.dot_general(
        left, right, (((1,), (1,)), ((), ())), preferred_element_type=jnp.float32
    ) + shift
    match = labels == lax.broadcasted_iota(jnp.int32, score.shape, text_axis) + first
    half = jax.nn.sigmoid(jnp.where(match, -score, score))
    return jnp.where(match, -half, half).astype(jnp.bfloat16)


def kernel(
    wide,
    narrow,
    scale_ref,
    shift_ref,
    label_hbm,
    image_hbm,
    text_hbm,
    grad_image_ref,
    grad_text_ref,
    image_ref,
    text_ref,
    texts,
    images,
    labels,
    label_column,
    label_ref,
    loaded,
    text_arrival,
    image_arrival,
    label_arrival,
    departure,
    label_departure,
):
    devices = wide * narrow
    me = lax.axis_index("wide") * narrow + lax.axis_index("narrow")
    odd = lax.rem(me, 2)
    rows = image_ref.shape[0]
    part = rows // CHUNKS

    def place(by):
        at = lax.rem(me + by + devices, devices)
        return (lax.div(at, narrow), lax.rem(at, narrow))

    column, row = lax.axis_index("wide"), lax.axis_index("narrow")
    low, top = row < 2, row >= narrow - 2

    def across(by):
        return (lax.rem(column + by + wide, wide), row)

    def tell(semaphore, device):
        pl.semaphore_signal(semaphore, inc=1, device_id=device, device_id_type=MESH)

    def either(test, yes, no):
        pl.when(test)(yes)
        pl.when(jnp.logical_not(test))(no)

    loads = [
        pltpu.make_async_copy(src, dst, loaded.at[at])
        for at, (src, dst) in enumerate(
            (
                (image_hbm, image_ref),
                (text_hbm, text_ref),
                (label_hbm, label_ref),
            )
        )
    ]
    barrier = pltpu.get_barrier_semaphore()
    tell(barrier, place(1 - 2 * odd))
    tell(barrier, place(2))
    tell(barrier, place(-2))
    for load in loads:
        load.start()
    pl.semaphore_wait(barrier, 3)
    for load in loads:
        load.wait()

    def routes(own_major, major, major_arrival, own_minor, minor, minor_arrival, d):
        def send(lane, src, dst, arrival, slot, by):
            def chunk(c, size=part):
                span = pl.ds(c * part, size)
                return pltpu.make_async_remote_copy(
                    src_ref=src.at[span],
                    dst_ref=dst.at[slot].at[span],
                    send_sem=departure.at[lane],
                    recv_sem=arrival.at[slot, c],
                    device_id=place(by),
                    device_id_type=MESH,
                )

            return chunk

        return (
            send(0, own_minor, minor, minor_arrival, 1, -2 * d),
            send(1, own_major, major, major_arrival, 1, 2 * d),
            send(2, own_major, major, major_arrival, 0, d),
            send(3, minor.at[1], minor, minor_arrival, 0, d),
            send(4, major.at[1], major, major_arrival, 2, d),
            send(5, major.at[0], major, major_arrival, 2, 2 * d),
        )

    text_side = (text_ref, texts, text_arrival)
    image_side = (image_ref, images, image_arrival)

    def both(body):
        @pl.when(odd == 0)
        def _():
            body(routes(*text_side, *image_side, 1), text_side, image_side)

        @pl.when(odd == 1)
        def _():
            body(routes(*image_side, *text_side, -1), image_side, text_side)

    def landed(side, slot, c):
        _, buffer, arrival = side
        here = buffer.at[slot].at[pl.ds(c * part, part)]
        pltpu.make_async_copy(here, here, arrival.at[slot, c]).wait()

    def label_lane(lane, src, slot, by):
        return pltpu.make_async_remote_copy(
            src_ref=src,
            dst_ref=labels.at[slot],
            send_sem=label_departure.at[lane],
            recv_sem=label_arrival.at[slot],
            device_id=place(by),
            device_id_type=MESH,
        )

    own_label = label_lane(0, label_ref, 1, -2)
    even_label = (label_lane(1, labels.at[1], 0, 1),)
    odd_label = (
        label_lane(1, label_ref, 0, -1),
        label_lane(2, labels.at[1], 2, -1),
        label_lane(3, labels.at[0], 2, -2),
    )

    def label_landed(slot):
        here = labels.at[slot]
        pltpu.make_async_copy(here, here, label_arrival.at[slot]).wait()

    def near_far(lanes, major):
        ahead, behind = (lanes[1], lanes[0]) if major is text_side else lanes[:2]
        return ahead, behind

    def begin(lanes, major, minor):
        ahead, behind = near_far(lanes, major)
        inner = jnp.logical_not(jnp.logical_or(low, top))
        pl.when(jnp.logical_not(low))(own_label.start)
        for c in range(CHUNKS):
            if c < HEAD:
                pl.when(jnp.logical_not(low))(behind(c).start)
                pl.when(jnp.logical_not(top))(ahead(c).start)
            else:

                @pl.when(inner)
                def _():
                    behind(c).start()
                    ahead(c).start()

            if c < AHEAD:
                lanes[2](c).start()
        if major is image_side:
            odd_label[0].start()

    def wrap(lanes, major, minor):
        ahead, behind = near_far(lanes, major)

        def mixed(far, near):
            for c in range(CHUNKS):
                far(c).start()
                if c + HEAD < CHUNKS:
                    near(c + HEAD).start()

        @pl.when(low)
        def _():
            own_label.start()
            mixed(behind, ahead)

        @pl.when(top)
        def _():
            mixed(ahead, behind)

    both(begin)
    both(wrap)

    scale, shift = scale_ref[0], shift_ref[0]
    label_column[...] = jnp.broadcast_to(label_ref[...], (rows, rows)).T

    def image_share(s, at=0, size=rows):
        span = pl.ds(at, size)
        block = text_ref[span] if s == 0 else texts[s - 1, span]
        slope = slope_tile(
            image_ref[...], block, label_column[:, :size], 1, s * rows + at, scale, shift
        )
        return scale * jnp.dot(slope, block, preferred_element_type=jnp.float32)

    def text_share(s, at=0, size=rows):
        span = pl.ds(at, size)
        block = image_ref[span] if s == 0 else images[s - 1, span]
        own = label_ref[:, span] if s == 0 else labels[s - 1, :, span]
        slope = slope_tile(text_ref[...], block, own, 0, s * rows, scale, shift)
        return scale * jnp.dot(slope, block, preferred_element_type=jnp.float32)

    def relay(*steps):
        def body(lanes, major, minor):
            source = {3: (minor, 1), 4: (major, 1), 5: (major, 0)}
            if major is text_side:
                tags = {(3, 0): (1, even_label[0])}
            else:
                tags = {(4, 0): (1, odd_label[1]), (5, 0): (0, odd_label[2])}
            for lane, c in steps:
                if (lane, c) in tags:
                    slot, copy = tags[lane, c]
                    label_landed(slot)
                    copy.start()
                if lane in source:
                    landed(*source[lane], c)
                lanes[lane](c).start()

        both(body)

    def add_text(s):
        grad_text_ref[...] += text_share(s)

    def add_image(s):
        grad_image_ref[...] += image_share(s)

    relay((3, 0), (2, 2))
    grad_image_ref[...] = image_share(0)
    relay((3, 1), (2, 3))
    grad_text_ref[...] = text_share(0)
    relay((4, 0), (3, 2), (4, 1), (3, 3), (4, 2), (5, 0), (4, 3), (5, 1), (5, 2), (5, 3))
    add_image(2)
    add_text(2)

    def rest(lanes, major, minor):
        for c in range(CHUNKS):
            landed(minor, 0, c)

    pl.when(odd == 0)(lambda: label_landed(0))
    label_landed(2)
    both(rest)
    add_image(1)
    add_text(1)

    def last(lanes, major, minor):
        for c in range(CHUNKS):
            landed(minor, 2, c)
        (add_text if major is text_side else add_image)(STEPS - 1)
        for c in range(CHUNKS):
            landed(major, 2, c)

    both(last)

    def finish(lanes, major, minor):
        for lane in lanes:
            lane(0, rows).wait_send()
        own_label.wait_send()
        for lane in even_label if major is text_side else odd_label:
            lane.wait_send()

    both(finish)


def tail_kernel(
    narrow,
    scale_ref,
    shift_ref,
    grad_image_ref,
    grad_text_ref,
    image_ref,
    text_ref,
    texts,
    images,
    labels,
    label_column,
    image_out,
    text_out,
    stage,
    stored,
):
    odd = lax.rem(lax.axis_index("wide") * narrow + lax.axis_index("narrow"), 2)
    scale, shift = scale_ref[0], shift_ref[0]
    rows = image_ref.shape[0]
    size, s = rows // PIECES, STEPS - 1

    def close(done, done_out, part_ref, out, own_ref, block_ref, slope_of):
        stores = [pltpu.make_async_copy(done, done_out, stored.at[PIECES])]
        stores[0].start()
        block = block_ref[s - 1]
        for piece in range(PIECES):
            span = pl.ds(piece * size, size)
            slope = slope_of(own_ref[span], block, piece * size, span)
            stage[span] = part_ref[span] + scale * jnp.dot(
                slope, block, preferred_element_type=jnp.float32
            )
            store = pltpu.make_async_copy(stage.at[span], out.at[span], stored.at[piece])
            store.start()
            stores.append(store)
        for store in stores:
            store.wait()

    @pl.when(odd == 0)
    def _():
        def slope_of(own, block, at, span):
            return slope_tile(own, block, label_column[span], 1, s * rows, scale, shift)

        close(grad_text_ref, text_out, grad_image_ref, image_out, image_ref, texts, slope_of)

    @pl.when(odd == 1)
    def _():
        def slope_of(own, block, at, span):
            return slope_tile(own, block, labels[s - 1], 0, s * rows + at, scale, shift)

        close(grad_image_ref, image_out, grad_text_ref, text_out, text_ref, images, slope_of)


def on_device(wide, narrow, photo, caption, match_index, logscale, offset):
    rows, width = photo.shape
    here = pl.BlockSpec(memory_space=pltpu.HBM)
    smem = pl.BlockSpec(memory_space=pltpu.SMEM)
    vmem = pl.BlockSpec(memory_space=pltpu.VMEM)
    operands = [
        pltpu.with_memory_space_constraint(array, pltpu.HBM)
        for array in (match_index.reshape(1, rows), photo, caption)
    ]
    held = (
        pltpu.VMEM((rows, width), jnp.float32),
        pltpu.VMEM((rows, width), jnp.float32),
        pltpu.VMEM((rows, width), jnp.bfloat16),
        pltpu.VMEM((rows, width), jnp.bfloat16),
        pltpu.VMEM((STEPS - 1, rows, width), jnp.bfloat16),
        pltpu.VMEM((STEPS - 1, rows, width), jnp.bfloat16),
        pltpu.VMEM((STEPS - 1, 1, rows), jnp.int32),
        pltpu.VMEM((rows, rows), jnp.int32),
    )
    tiles = 4 * STEPS * rows * rows * width
    results = pl.pallas_call(
        functools.partial(kernel, wide, narrow),
        out_shape=held,
        in_specs=[smem] * 2 + [here] * 3,
        out_specs=(vmem,) * len(held),
        scratch_shapes=[
            pltpu.VMEM((1, rows), jnp.int32),
            pltpu.SemaphoreType.DMA((3,)),
            pltpu.SemaphoreType.DMA((STEPS - 1, CHUNKS)),
            pltpu.SemaphoreType.DMA((STEPS - 1, CHUNKS)),
            pltpu.SemaphoreType.DMA((STEPS - 1,)),
            pltpu.SemaphoreType.DMA((6,)),
            pltpu.SemaphoreType.DMA((4,)),
        ],
        compiler_params=pltpu.CompilerParams(
            collective_id=0, has_side_effects=True, vmem_limit_bytes=32 * 1024 * 1024
        ),
        cost_estimate=pl.CostEstimate(
            flops=2 * tiles, bytes_accessed=6 * rows * width * 2, transcendentals=0
        ),
        name="sigmoid_ring",
    )(logscale, offset, *operands)
    out = jax.ShapeDtypeStruct((rows, width), jnp.float32)
    return pl.pallas_call(
        functools.partial(tail_kernel, narrow),
        out_shape=(out, out),
        in_specs=[smem] * 2 + [vmem] * len(held),
        out_specs=(here, here),
        scratch_shapes=[
            pltpu.VMEM((rows, width), jnp.float32),
            pltpu.SemaphoreType.DMA((PIECES + 1,)),
        ],
        compiler_params=pltpu.CompilerParams(vmem_limit_bytes=16 * 1024 * 1024),
        name="sigmoid_tail",
    )(logscale, offset, *results)


def solution(mesh):
    pairs = ("wide", "narrow")
    return jax.shard_map(
        functools.partial(on_device, mesh.shape["wide"], mesh.shape["narrow"]),
        mesh=mesh,
        in_specs=(P(pairs, None), P(pairs, None), P(pairs), P(), P()),
        out_specs=(P(pairs, None), P(pairs, None)),
        check_vma=False,
    )
```

```python
import functools

import jax
import jax.numpy as jnp
from jax import lax
from jax.experimental import pallas as pl
from jax.experimental.pallas import tpu as pltpu
from jax.sharding import PartitionSpec as P

STEPS = 4
CHUNKS = 4
AHEAD = 2
PIECES = 4
HEAD = 0
MESH = pl.DeviceIdType.MESH


def slope_tile(left, right, labels, text_axis, first, scale, shift):
    score = scale * lax.dot_general(
        left, right, (((1,), (1,)), ((), ())), preferred_element_type=jnp.float32
    ) + shift
    match = labels == lax.broadcasted_iota(jnp.int32, score.shape, text_axis) + first
    half = jax.nn.sigmoid(jnp.where(match, -score, score))
    return jnp.where(match, -half, half).astype(jnp.bfloat16)


def kernel(
    wide,
    narrow,
    scale_ref,
    shift_ref,
    label_hbm,
    image_hbm,
    text_hbm,
    grad_image_ref,
    grad_text_ref,
    image_ref,
    text_ref,
    texts,
    images,
    labels,
    label_column,
    label_ref,
    loaded,
    text_arrival,
    image_arrival,
    label_arrival,
    departure,
    label_departure,
):
    devices = wide * narrow
    me = lax.axis_index("wide") * narrow + lax.axis_index("narrow")
    odd = lax.rem(me, 2)
    rows = image_ref.shape[0]
    part = rows // CHUNKS

    def place(by):
        at = lax.rem(me + by + devices, devices)
        return (lax.div(at, narrow), lax.rem(at, narrow))

    column, row = lax.axis_index("wide"), lax.axis_index("narrow")
    low, top = row < 2, row >= narrow - 2

    def across(by):
        return (lax.rem(column + by + wide, wide), row)

    def tell(semaphore, device):
        pl.semaphore_signal(semaphore, inc=1, device_id=device, device_id_type=MESH)

    def either(test, yes, no):
        pl.when(test)(yes)
        pl.when(jnp.logical_not(test))(no)

    loads = [
        pltpu.make_async_copy(src, dst, loaded.at[at])
        for at, (src, dst) in enumerate(
            (
                (image_hbm, image_ref),
                (text_hbm, text_ref),
                (label_hbm, label_ref),
            )
        )
    ]
    barrier = pltpu.get_barrier_semaphore()
    tell(barrier, place(1 - 2 * odd))
    tell(barrier, place(2))
    tell(barrier, place(-2))
    for load in loads:
        load.start()
    pl.semaphore_wait(barrier, 3)
    for load in loads:
        load.wait()

    def routes(own_major, major, major_arrival, own_minor, minor, minor_arrival, d):
        def send(lane, src, dst, arrival, slot, by):
            def chunk(c, size=part):
                span = pl.ds(c * part, size)
                return pltpu.make_async_remote_copy(
                    src_ref=src.at[span],
                    dst_ref=dst.at[slot].at[span],
                    send_sem=departure.at[lane],
                    recv_sem=arrival.at[slot, c],
                    device_id=place(by),
                    device_id_type=MESH,
                )

            return chunk

        return (
            send(0, own_minor, minor, minor_arrival, 1, -2 * d),
            send(1, own_major, major, major_arrival, 1, 2 * d),
            send(2, own_major, major, major_arrival, 0, d),
            send(3, minor.at[1], minor, minor_arrival, 0, d),
            send(4, major.at[1], major, major_arrival, 2, d),
            send(5, major.at[0], major, major_arrival, 2, 2 * d),
        )

    text_side = (text_ref, texts, text_arrival)
    image_side = (image_ref, images, image_arrival)

    def both(body):
        @pl.when(odd == 0)
        def _():
            body(routes(*text_side, *image_side, 1), text_side, image_side)

        @pl.when(odd == 1)
        def _():
            body(routes(*image_side, *text_side, -1), image_side, text_side)

    def landed(side, slot, c):
        _, buffer, arrival = side
        here = buffer.at[slot].at[pl.ds(c * part, part)]
        pltpu.make_async_copy(here, here, arrival.at[slot, c]).wait()

    def label_lane(lane, src, slot, by):
        return pltpu.make_async_remote_copy(
            src_ref=src,
            dst_ref=labels.at[slot],
            send_sem=label_departure.at[lane],
            recv_sem=label_arrival.at[slot],
            device_id=place(by),
            device_id_type=MESH,
        )

    own_label = label_lane(0, label_ref, 1, -2)
    even_label = (label_lane(1, labels.at[1], 0, 1),)
    odd_label = (
        label_lane(1, label_ref, 0, -1),
        label_lane(2, labels.at[1], 2, -1),
        label_lane(3, labels.at[0], 2, -2),
    )

    def label_landed(slot):
        here = labels.at[slot]
        pltpu.make_async_copy(here, here, label_arrival.at[slot]).wait()

    def near_far(lanes, major):
        ahead, behind = (lanes[1], lanes[0]) if major is text_side else lanes[:2]
        return ahead, behind

    def begin(lanes, major, minor):
        ahead, behind = near_far(lanes, major)
        inner = jnp.logical_not(jnp.logical_or(low, top))
        pl.when(jnp.logical_not(low))(own_label.start)
        for c in range(CHUNKS):
            if c < HEAD:
                pl.when(jnp.logical_not(low))(behind(c).start)
                pl.when(jnp.logical_not(top))(ahead(c).start)
            else:

                @pl.when(inner)
                def _():
                    behind(c).start()
                    ahead(c).start()

            if c < AHEAD:
                lanes[2](c).start()
        if major is image_side:
            odd_label[0].start()

    def wrap(lanes, major, minor):
        ahead, behind = near_far(lanes, major)

        def mixed(far, near):
            for c in range(CHUNKS):
                far(c).start()
                if c + HEAD < CHUNKS:
                    near(c + HEAD).start()

        @pl.when(low)
        def _():
            own_label.start()
            mixed(behind, ahead)

        @pl.when(top)
        def _():
            mixed(ahead, behind)

    both(begin)
    both(wrap)

    scale, shift = scale_ref[0], shift_ref[0]
    label_column[...] = jnp.broadcast_to(label_ref[...], (rows, rows)).T

    def image_share(s, at=0, size=rows):
        span = pl.ds(at, size)
        block = text_ref[span] if s == 0 else texts[s - 1, span]
        slope = slope_tile(
            image_ref[...], block, label_column[:, :size], 1, s * rows + at, scale, shift
        )
        return scale * jnp.dot(slope, block, preferred_element_type=jnp.float32)

    def text_share(s, at=0, size=rows):
        span = pl.ds(at, size)
        block = image_ref[span] if s == 0 else images[s - 1, span]
        own = label_ref[:, span] if s == 0 else labels[s - 1, :, span]
        slope = slope_tile(text_ref[...], block, own, 0, s * rows, scale, shift)
        return scale * jnp.dot(slope, block, preferred_element_type=jnp.float32)

    def relay(*steps):
        def body(lanes, major, minor):
            source = {3: (minor, 1), 4: (major, 1), 5: (major, 0)}
            if major is text_side:
                tags = {(3, 0): (1, even_label[0])}
            else:
                tags = {(4, 0): (1, odd_label[1]), (5, 0): (0, odd_label[2])}
            for lane, c in steps:
                if (lane, c) in tags:
                    slot, copy = tags[lane, c]
                    label_landed(slot)
                    copy.start()
                if lane in source:
                    landed(*source[lane], c)
                lanes[lane](c).start()

        both(body)

    def add_text(s):
        grad_text_ref[...] += text_share(s)

    def add_image(s):
        grad_image_ref[...] += image_share(s)

    relay((3, 0), (2, 2))
    grad_image_ref[...] = image_share(0)
    relay((3, 1), (2, 3))
    grad_text_ref[...] = text_share(0)
    relay((4, 0), (3, 2), (4, 1), (3, 3), (4, 2), (5, 0), (4, 3), (5, 1), (5, 2), (5, 3))
    add_image(2)
    add_text(2)

    def rest(lanes, major, minor):
        for c in range(CHUNKS):
            landed(minor, 0, c)

    pl.when(odd == 0)(lambda: label_landed(0))
    label_landed(2)
    both(rest)
    add_image(1)
    add_text(1)

    def last(lanes, major, minor):
        for c in range(CHUNKS):
            landed(minor, 2, c)
        (add_text if major is text_side else add_image)(STEPS - 1)
        for c in range(CHUNKS):
            landed(major, 2, c)

    both(last)

    def finish(lanes, major, minor):
        for lane in lanes:
            lane(0, rows).wait_send()
        own_label.wait_send()
        for lane in even_label if major is text_side else odd_label:
            lane.wait_send()

    both(finish)


def tail_kernel(
    narrow,
    scale_ref,
    shift_ref,
    grad_image_ref,
    grad_text_ref,
    image_ref,
    text_ref,
    texts,
    images,
    labels,
    label_column,
    image_out,
    text_out,
    stage,
    stored,
):
    odd = lax.rem(lax.axis_index("wide") * narrow + lax.axis_index("narrow"), 2)
    scale, shift = scale_ref[0], shift_ref[0]
    rows, width = image_ref.shape
    s = STEPS - 1
    cuts = [width * piece // PIECES // 256 * 256 for piece in range(PIECES)] + [width]

    def close(done, done_out, part_ref, out, own_ref, block_ref, slope_of):
        stores = [pltpu.make_async_copy(done, done_out, stored.at[PIECES])]
        stores[0].start()
        block = block_ref.at[s - 1]
        slope = slope_of(own_ref[...], block[...])
        for piece in range(PIECES):
            at = pl.ds(cuts[piece], cuts[piece + 1] - cuts[piece])
            stage[:, at] = part_ref[:, at] + scale * jnp.dot(
                slope, block[:, at], preferred_element_type=jnp.float32
            )
            store = pltpu.make_async_copy(stage.at[:, at], out.at[:, at], stored.at[piece])
            store.start()
            stores.append(store)
        for store in stores:
            store.wait()

    @pl.when(odd == 0)
    def _():
        def slope_of(own, block):
            return slope_tile(own, block, label_column[...], 1, s * rows, scale, shift)

        close(grad_text_ref, text_out, grad_image_ref, image_out, image_ref, texts, slope_of)

    @pl.when(odd == 1)
    def _():
        def slope_of(own, block):
            return slope_tile(own, block, labels[s - 1], 0, s * rows, scale, shift)

        close(grad_image_ref, image_out, grad_text_ref, text_out, text_ref, images, slope_of)


def on_device(wide, narrow, photo, caption, match_index, logscale, offset):
    rows, width = photo.shape
    here = pl.BlockSpec(memory_space=pltpu.HBM)
    smem = pl.BlockSpec(memory_space=pltpu.SMEM)
    vmem = pl.BlockSpec(memory_space=pltpu.VMEM)
    operands = [
        pltpu.with_memory_space_constraint(array, pltpu.HBM)
        for array in (match_index.reshape(1, rows), photo, caption)
    ]
    held = (
        pltpu.VMEM((rows, width), jnp.float32),
        pltpu.VMEM((rows, width), jnp.float32),
        pltpu.VMEM((rows, width), jnp.bfloat16),
        pltpu.VMEM((rows, width), jnp.bfloat16),
        pltpu.VMEM((STEPS - 1, rows, width), jnp.bfloat16),
        pltpu.VMEM((STEPS - 1, rows, width), jnp.bfloat16),
        pltpu.VMEM((STEPS - 1, 1, rows), jnp.int32),
        pltpu.VMEM((rows, rows), jnp.int32),
    )
    tiles = 4 * STEPS * rows * rows * width
    results = pl.pallas_call(
        functools.partial(kernel, wide, narrow),
        out_shape=held,
        in_specs=[smem] * 2 + [here] * 3,
        out_specs=(vmem,) * len(held),
        scratch_shapes=[
            pltpu.VMEM((1, rows), jnp.int32),
            pltpu.SemaphoreType.DMA((3,)),
            pltpu.SemaphoreType.DMA((STEPS - 1, CHUNKS)),
            pltpu.SemaphoreType.DMA((STEPS - 1, CHUNKS)),
            pltpu.SemaphoreType.DMA((STEPS - 1,)),
            pltpu.SemaphoreType.DMA((6,)),
            pltpu.SemaphoreType.DMA((4,)),
        ],
        compiler_params=pltpu.CompilerParams(
            collective_id=0, has_side_effects=True, vmem_limit_bytes=32 * 1024 * 1024
        ),
        cost_estimate=pl.CostEstimate(
            flops=2 * tiles, bytes_accessed=6 * rows * width * 2, transcendentals=0
        ),
        name="sigmoid_ring",
    )(logscale, offset, *operands)
    out = jax.ShapeDtypeStruct((rows, width), jnp.float32)
    return pl.pallas_call(
        functools.partial(tail_kernel, narrow),
        out_shape=(out, out),
        in_specs=[smem] * 2 + [vmem] * len(held),
        out_specs=(here, here),
        scratch_shapes=[
            pltpu.VMEM((rows, width), jnp.float32),
            pltpu.SemaphoreType.DMA((PIECES + 1,)),
        ],
        compiler_params=pltpu.CompilerParams(vmem_limit_bytes=16 * 1024 * 1024),
        name="sigmoid_tail",
    )(logscale, offset, *results)


def solution(mesh):
    pairs = ("wide", "narrow")
    return jax.shard_map(
        functools.partial(on_device, mesh.shape["wide"], mesh.shape["narrow"]),
        mesh=mesh,
        in_specs=(P(pairs, None), P(pairs, None), P(pairs), P(), P()),
        out_specs=(P(pairs, None), P(pairs, None)),
        check_vma=False,
    )
```
